32 devices in a mesh: bl: 8 (over y, x, core), ch: 4 (over z).
Axes of the slice: x: 2, y: 2, z: 4, core: 2. Of those that a mesh axis runs over, the one named last changes fastest.
Arguments:
- measured_correlations: float32 [2, 64, 16384], P(None, 'ch', 'bl'), may hold values from -6 to 6
- source_model_terms: float32 [2, 16, 64, 16384], P(None, None, 'ch', 'bl'), may hold values from -0.75 to 0.75
- stations: int32 [2, 16384], P(None, 'bl'), may hold values from 0 to 511, as said below
- initial_gains: float32 [2, 16, 64, 512], P(None, None, 'ch'), may hold values from -4 to 4
Outputs:
- gains: float32 [2, 16, 64, 512], P(None, None, 'ch')
- consensus: float32 [2, 16, 64, 512], P(None, None, 'ch')
The draws below stay inside these ranges and needn't reach their ends.
Inputs may be any that keep to these rules, and one draw needn't show every extreme that they name: Each baseline joins two different stations.
All inputs are finite; a program needn't handle non-finite values.
Results may differ from the reference program's by a relative error of at most 0.00025.
Values sent between devices are 32-bit elements; how exact they have to be, the bound alone decides.
A program may use at most 64 MiB of HBM per device.

```python
import jax
import jax.numpy as jnp
from jax import lax

RECEIVER_SITES = 512
SOURCE_PATCHES = 16
SPECTRAL_BINS = 64
PAIR_PORTION = 2048
ITERS = 3
PAIR_COUNT_ALL = 16384
N_BL = 8


def draw_stations(key, part):
    pair_start_receiver, pair_end_receiver = jax.random.split(key)
    start_receiver_number = jax.random.randint(pair_start_receiver, (PAIR_COUNT_ALL,), 0, RECEIVER_SITES)
    portion_starts = jax.random.randint(pair_end_receiver, (PAIR_COUNT_ALL,), 1, RECEIVER_SITES)
    right_ids = (start_receiver_number + portion_starts) % RECEIVER_SITES
    start_receiver_number = start_receiver_number.at[0].set(0)
    right_ids = right_ids.at[0].set(RECEIVER_SITES - 1)
    return jnp.stack([start_receiver_number, right_ids]).astype(jnp.int32)


def shard_levels(key, extent, cuts, smallest, top_value):
    def one(dim, shards_of):
        draws = jax.random.uniform(jax.random.fold_in(jax.random.fold_in(key, 6), dim), (shards_of,), jnp.float32, smallest / len(cuts), top_value / len(cuts))
        return jnp.repeat(jnp.exp(draws), extent[dim] // shards_of).reshape((-1,) + (1,) * (len(extent) - dim - 1))

    level = one(*cuts[0])
    for cut in cuts[1:]:
        level = level * one(*cut)
    return level


def gaussian(rng, extent, spread, bound, shards=(), kind=jnp.bfloat16):
    level = shard_levels(rng, extent, shards, -0.22, 0.18) if shards else 1.0
    array = jax.random.normal(rng, extent, jnp.float32) * spread * level
    return jnp.minimum(jnp.maximum(array, -bound), bound).astype(kind)


def setup_inputs(seed: int = 0) -> dict:
    arg_keys = jax.random.split(jax.random.key(seed), 5)
    return {
        "measured_correlations": gaussian(arg_keys[0], (2, SPECTRAL_BINS, PAIR_COUNT_ALL), 1.0, 6.0, ((1, 4), (2, 8)), jnp.float32),
        "source_model_terms": gaussian(arg_keys[1], (2, SOURCE_PATCHES, SPECTRAL_BINS, PAIR_COUNT_ALL), (2 * PAIR_PORTION * N_BL // RECEIVER_SITES) ** -0.5, 0.75, ((2, 4), (3, 8)), jnp.float32),
        "stations": draw_stations(jax.random.fold_in(arg_keys[4], 71), 0),
        "initial_gains": gaussian(arg_keys[3], (2, SOURCE_PATCHES, SPECTRAL_BINS, RECEIVER_SITES), 1.0, 4.0, ((2, 4),), jnp.float32),
    }


penalty = 1.0

def legendre_basis(channel_count):
    abscissa = -1.0 + 2.0 * jnp.arange(channel_count, dtype=jnp.float32) / (channel_count - 1)
    columns = []
    for degree in range(4):
        vector = abscissa ** degree
        for earlier in columns:
            vector = vector - jnp.sum(earlier * vector) * earlier
        vector = vector / jnp.sqrt(jnp.sum(vector * vector))
        columns.append(vector)
    return jnp.stack(columns, axis=1)

def complex_terms(measured_correlations, source_model_terms, gain_left, gain_right):
    m_real, m_imag = (source_model_terms[0], source_model_terms[1])
    left_re, left_im = (gain_left[0], gain_left[1])
    right_re, right_im = (gain_right[0], gain_right[1])
    a_real = m_real * right_re + m_imag * right_im
    a_imag = m_imag * right_re - m_real * right_im
    pred_re = left_re * a_real - left_im * a_imag
    pred_im = left_re * a_imag + left_im * a_real
    resid_re = measured_correlations[0] - lax.optimization_barrier(jnp.sum(pred_re, axis=0))
    resid_im = measured_correlations[1] - lax.optimization_barrier(jnp.sum(pred_im, axis=0))
    y_real = resid_re[None] + pred_re
    y_imag = resid_im[None] + pred_im
    left_terms = jnp.stack([y_real * a_real + y_imag * a_imag, y_imag * a_real - y_real * a_imag, a_real * a_real + a_imag * a_imag])
    b_real = m_real * left_re - m_imag * left_im
    b_imag = m_real * left_im + m_imag * left_re
    right_terms = jnp.stack([y_real * b_real + y_imag * b_imag, y_real * b_imag - y_imag * b_real, b_real * b_real + b_imag * b_imag])
    return (left_terms, right_terms)

def update_gains(totals, consensus, dual):
    factor = 1.0 / (totals[2] + penalty)
    return jnp.stack([(totals[0] + penalty * (consensus[0] - dual[0])) * factor, (totals[1] + penalty * (consensus[1] - dual[1])) * factor])

def station_scatter(terms, station_ids):
    moved = jnp.moveaxis(terms, 3, 0)
    summed = jax.ops.segment_sum(moved, station_ids, num_segments=RECEIVER_SITES)
    return jnp.moveaxis(summed, 0, 3)

def reference(measured_correlations, source_model_terms, stations, initial_gains):
    basis = legendre_basis(SPECTRAL_BINS)
    gains = initial_gains
    consensus = initial_gains
    dual = jnp.zeros_like(initial_gains)
    start_receiver_number = stations[0]
    right_ids = stations[1]
    for iteration in range(ITERS):
        gain_left = jnp.take(gains, start_receiver_number, axis=3)
        gain_right = jnp.take(gains, right_ids, axis=3)
        left_terms, right_terms = complex_terms(measured_correlations, source_model_terms, gain_left, gain_right)
        totals = station_scatter(left_terms, start_receiver_number) + station_scatter(right_terms, right_ids)
        gains = update_gains(totals, consensus, dual)
        shifted = gains + dual
        coeffs = jnp.einsum('fk,rdfs->rdks', basis, shifted, precision=lax.Precision.HIGHEST)
        consensus = jnp.einsum('fk,rdks->rdfs', basis, coeffs, precision=lax.Precision.HIGHEST)
        dual = shifted - consensus
    return (gains, consensus)
```

```python
import functools

import jax
import jax.numpy as jnp
import numpy as np
from jax import lax
from jax.experimental import pallas as pl
from jax.experimental.pallas import tpu as pltpu
from jax.sharding import PartitionSpec as P

SPECTRAL_BINS = 64
ITERS = 3
penalty = 1.0
MESH = pl.DeviceIdType.MESH
BLOCK = 512


def legendre_basis(channel_count):
    abscissa = -1.0 + 2.0 * jnp.arange(channel_count, dtype=jnp.float32) / (channel_count - 1)
    columns = []
    for degree in range(4):
        vector = abscissa**degree
        for earlier in columns:
            vector = vector - jnp.sum(earlier * vector) * earlier
        vector = vector / jnp.sqrt(jnp.sum(vector * vector))
        columns.append(vector)
    return jnp.stack(columns, axis=1)


def split(value):
    high = value.astype(jnp.bfloat16)
    return high, (value - high.astype(jnp.float32)).astype(jnp.bfloat16)


def totals_kernel(
    n_chunks, n_dir, n_chan, vis_ref, model_ref, row_ref, col_ref, gains_ref, out_ref,
    pieces, gain_l, gain_r, terms, back, accum,
):
    step = pl.program_id(0)
    rows = n_dir * n_chan
    chunk = rows // n_chunks
    block = vis_ref.shape[2]
    n_st = pieces.shape[1]
    half = n_st // 2

    @pl.when(step == 0)
    def _():
        for h in range(2):
            for c in range(n_chunks):
                for part in range(2):
                    high, low = split(gains_ref[h, c, pl.ds(part * chunk, chunk), :])
                    base = part * rows + c * chunk
                    pieces[pl.ds(base, chunk), pl.ds(h * half, half)] = high
                    pieces[pl.ds(2 * rows + base, chunk), pl.ds(h * half, half)] = low

    station = lax.broadcasted_iota(jnp.int32, (n_st, block), 0)
    hot_l = (station == row_ref[0:1, :]).astype(jnp.float32).astype(jnp.bfloat16)
    hot_r = (station == row_ref[1:2, :]).astype(jnp.float32).astype(jnp.bfloat16)
    for hot, gain in ((hot_l, gain_l), (hot_r, gain_r)):
        both = jnp.dot(pieces[...], hot, preferred_element_type=jnp.float32)
        gain[...] = both[: 2 * rows] + both[2 * rows :]

    def at(ref, part, d):
        return ref[pl.ds(part * rows + d * n_chan, n_chan), :]

    res_re = vis_ref[0]
    res_im = vis_ref[1]
    for d in range(n_dir):
        m_re, m_im = model_ref[0, d], model_ref[1, d]
        l_re, l_im = at(gain_l, 0, d), at(gain_l, 1, d)
        r_re, r_im = at(gain_r, 0, d), at(gain_r, 1, d)
        a_re = m_re * r_re + m_im * r_im
        a_im = m_im * r_re - m_re * r_im
        res_re = res_re - (l_re * a_re - l_im * a_im)
        res_im = res_im - (l_re * a_im + l_im * a_re)
    for d in range(n_dir):
        m_re, m_im = model_ref[0, d], model_ref[1, d]
        t_re = res_re * m_re + res_im * m_im
        t_im = res_re * m_im - res_im * m_re
        power = m_re * m_re + m_im * m_im
        for side, gain in ((0, gain_r), (1, gain_l)):
            g_re, g_im = at(gain, 0, d), at(gain, 1, d)
            sign = -1.0 if side == 0 else 1.0
            s_im = sign * t_im
            values = (
                t_re * g_re - s_im * g_im,
                t_re * g_im + s_im * g_re,
                power * (g_re * g_re + g_im * g_im),
            )
            for q, value in enumerate(values):
                high, low = split(value)
                base = q * rows + d * n_chan
                terms[pl.ds(base, n_chan), pl.ds(pl.multiple_of((step * 2 + side) * block, 128), block)] = high
                terms[pl.ds(3 * rows + base, n_chan), pl.ds(pl.multiple_of((step * 2 + side) * block, 128), block)] = low

    ids = lax.broadcasted_iota(jnp.int32, (block, n_st), 1)
    back_l = (ids == col_ref[:, 0:1]).astype(jnp.float32).astype(jnp.bfloat16)
    back_r = (ids == col_ref[:, 1:2]).astype(jnp.float32).astype(jnp.bfloat16)
    back[pl.ds(step * 2 * block, block), :] = back_l
    back[pl.ds(step * 2 * block + block, block), :] = back_r

    @pl.when(step == pl.num_programs(0) - 1)
    def _():
        accum[...] = jnp.dot(terms[...], back[...], preferred_element_type=jnp.float32)
        for h in range(2):
            for c in range(n_chunks):
                for q in range(3):
                    base = q * rows + c * chunk
                    out_ref[h, c, pl.ds(q * chunk, chunk), :] = (
                        accum[pl.ds(base, chunk), pl.ds(h * half, half)]
                        + accum[pl.ds(3 * rows + base, chunk), pl.ds(h * half, half)]
                    )


def local_totals(vis, model, ids, ids_t, gains, n_chunks):
    n_dir, n_chan, n_base = model.shape[1:]
    n_st = gains.shape[3] * 2
    rows = n_dir * n_chan
    chunk = rows // n_chunks
    block = min(BLOCK, n_base)
    return pl.pallas_call(
        functools.partial(totals_kernel, n_chunks, n_dir, n_chan),
        grid=(n_base // block,),
        out_shape=jax.ShapeDtypeStruct((2, n_chunks, 3 * chunk, n_st // 2), jnp.float32),
        in_specs=[
            pl.BlockSpec((2, n_chan, block), lambda i: (0, 0, i)),
            pl.BlockSpec((2, n_dir, n_chan, block), lambda i: (0, 0, 0, i)),
            pl.BlockSpec((2, block), lambda i: (0, i)),
            pl.BlockSpec((block, 2), lambda i: (i, 0)),
            pl.BlockSpec(gains.shape, lambda i: (0, 0, 0, 0)),
        ],
        out_specs=pl.BlockSpec((2, n_chunks, 3 * chunk, n_st // 2), lambda i: (0, 0, 0, 0)),
        scratch_shapes=[
            pltpu.VMEM((4 * rows, n_st), jnp.bfloat16),
            pltpu.VMEM((2 * rows, block), jnp.float32),
            pltpu.VMEM((2 * rows, block), jnp.float32),
            pltpu.VMEM((6 * rows, 2 * n_base), jnp.bfloat16),
            pltpu.VMEM((2 * n_base, n_st), jnp.bfloat16),
            pltpu.VMEM((6 * rows, n_st), jnp.float32),
        ],
        compiler_params=pltpu.CompilerParams(vmem_limit_bytes=56 * 2**20),
        name="station_totals",
    )(vis, model, ids, ids_t, gains)


def orders(n_bits):
    upper = list(range(1, n_bits))
    return ([0] + upper, [0] + upper[::-1])


def exchange_kernel(
    last, n_bits, n_ch, part_ref, state_ref, basis_ref, gains_ref, out_state_ref, coef_all_ref,
    acc, recv, coefs, sem_in, rs_send, rs_recv, ag_send, ag_recv, c_send, c_recv, k_send, k_recv,
):
    n = 2**n_bits
    rows = state_ref.shape[2]
    me = lax.axis_index("bl")
    ch = lax.axis_index("ch")
    bits = [lax.rem(me // (2**k), 2) for k in range(n_bits)]
    partners = [me + (1 - 2 * bits[k]) * (2**k) for k in range(n_bits)]
    load = pltpu.make_async_copy(part_ref, acc, sem_in)
    load.start()

    barrier = pltpu.get_barrier_semaphore()
    for k in range(n_bits):
        pl.semaphore_signal(barrier, inc=1, device_id=(partners[k], ch), device_id_type=MESH)
    for j in range(1, n_ch):
        pl.semaphore_signal(
            barrier, inc=1, device_id=(me, lax.rem(ch + j, n_ch)), device_id_type=MESH
        )
    pl.semaphore_wait(barrier, n_bits + n_ch - 1)
    load.wait()

    order = orders(n_bits)

    def region(stream, stage, flip):
        idx = [slice(None)] * n_bits
        for j in range(stage):
            k = order[stream][j]
            idx[n_bits - 1 - k] = bits[k]
        k = order[stream][stage]
        idx[n_bits - 1 - k] = (1 - bits[k]) if flip else bits[k]
        return (stream,) + tuple(idx)

    def rs_copy(stream, stage):
        k = order[stream][stage]
        slot = recv[stage].at[stream]
        return pltpu.make_async_remote_copy(
            src_ref=acc.at[region(stream, stage, True)],
            dst_ref=slot,
            send_sem=rs_send.at[stream, stage],
            recv_sem=rs_recv.at[stream, stage],
            device_id=(partners[k], ch),
            device_id_type=MESH,
        )

    copies = {}
    for s in range(2):
        copies[s, 0] = rs_copy(s, 0)
        copies[s, 0].start()
    for stage in range(n_bits):
        for s in range(2):
            copies[s, stage].wait_recv()
            where = region(s, stage, False)
            acc[where] = acc[where] + recv[stage][s]
            if stage + 1 < n_bits:
                copies[s, stage + 1] = rs_copy(s, stage + 1)
                copies[s, stage + 1].start()

    mine = tuple(bits[n_bits - 1 - i] for i in range(n_bits))

    def gather_copy(buf, sends, recvs, stream, stage):
        k = order[stream][stage]
        idx = [slice(None)] * n_bits
        for j in range(stage + 1):
            kk = order[stream][j]
            idx[n_bits - 1 - kk] = bits[kk]
        where = (stream,) + tuple(idx)
        return pltpu.make_async_remote_copy(
            src_ref=buf.at[where],
            dst_ref=buf.at[where],
            send_sem=sends.at[stream, stage],
            recv_sem=recvs.at[stream, stage],
            device_id=(partners[k], ch),
            device_id_type=MESH,
        )

    gathers = {}
    shifted = []
    for s in range(2):
        totals = acc[(s,) + mine]
        weight = totals[2 * rows :]
        factor = 1.0 / (weight + penalty)
        for part in range(2):
            gain = state_ref[0, s * 2 + part]
            cons = state_ref[1, s * 2 + part]
            dual = state_ref[2, s * 2 + part]
            numerator = totals[part * rows : (part + 1) * rows] + gain * weight
            new = (numerator + penalty * (cons - dual)) * factor
            gains_ref[(s,) + mine + (pl.ds(part * rows, rows),)] = new
            out_state_ref[0, s * 2 + part] = new
            shifted.append(new + dual)
        gathers[s, n_bits - 1] = gather_copy(gains_ref, ag_send, ag_recv, s, n_bits - 1)
        gathers[s, n_bits - 1].start()

    n_chan = basis_ref.shape[1]
    per = rows // n_chan
    for k in range(4):
        pieces = []
        for value in shifted:
            for i in range(per):
                pieces.append(
                    jnp.sum(
                        value[i * n_chan : (i + 1) * n_chan] * basis_ref[k], axis=0, keepdims=True
                    )
                )
        for r, piece in enumerate(pieces):
            coefs[0, k, pl.ds(r, 1), :] = piece
    sends = []
    for j in range(1, n_ch):
        copy = pltpu.make_async_remote_copy(
            src_ref=coefs.at[0],
            dst_ref=coefs.at[j],
            send_sem=c_send.at[j - 1],
            recv_sem=c_recv.at[j - 1],
            device_id=(me, lax.rem(ch + j, n_ch)),
            device_id_type=MESH,
        )
        copy.start()
        sends.append(copy)

    def advance(buf, sends, recvs, table, stage):
        for s in range(2):
            table[s, stage].wait_recv()
            if stage > 0:
                table[s, stage - 1] = gather_copy(buf, sends, recvs, s, stage - 1)
                table[s, stage - 1].start()

    advance(gains_ref, ag_send, ag_recv, gathers, n_bits - 1)
    for copy in sends:
        copy.wait_recv()
    total = [None] * 4
    for k in range(4):
        value = coefs[0, k]
        for j in range(1, n_ch):
            value = value + coefs[j, k]
        total[k] = value
    k_gathers = {}
    if last:
        for s in range(2):
            for k in range(4):
                coef_all_ref[(s,) + mine + (k,)] = total[k][s * 2 * per : (s + 1) * 2 * per]
            k_gathers[s, n_bits - 1] = gather_copy(coef_all_ref, k_send, k_recv, s, n_bits - 1)
            k_gathers[s, n_bits - 1].start()
        out_state_ref[1] = out_state_ref[0]
        out_state_ref[2] = out_state_ref[0]
    else:
        coef_all_ref[...] = jnp.zeros_like(coef_all_ref)
        for index, value in enumerate(shifted):
            for i in range(per):
                fit = total[0][index * per + i : index * per + i + 1] * basis_ref[0]
                for k in range(1, 4):
                    fit = fit + total[k][index * per + i : index * per + i + 1] * basis_ref[k]
                where = pl.ds(i * n_chan, n_chan)
                out_state_ref[1, index, where, :] = fit
                out_state_ref[2, index, where, :] = value[i * n_chan : (i + 1) * n_chan] - fit
    for stage in range(n_bits - 2, -1, -1):
        advance(gains_ref, ag_send, ag_recv, gathers, stage)
        if last:
            advance(coef_all_ref, k_send, k_recv, k_gathers, stage + 1)
    if last:
        advance(coef_all_ref, k_send, k_recv, k_gathers, 0)

    for table in (copies, gathers, k_gathers):
        for copy in table.values():
            copy.wait_send()
    for copy in sends:
        copy.wait_send()


def exchange(partial, state, basis, last, n, n_ch):
    n_bits = n.bit_length() - 1
    rows, half = state.shape[2:]
    n_chan = basis.shape[1]
    per = rows // n_chan
    twos = (2,) * n_bits
    partial = partial.reshape((2,) + twos + partial.shape[2:])
    coef_shape = (2,) + ((twos) if last else (1,) * n_bits) + (4, 2 * per, half)
    recv = [
        pltpu.VMEM((2,) + (2,) * (n_bits - 1 - stage) + (3 * rows, half), jnp.float32)
        for stage in range(n_bits)
    ]

    def body(part_ref, state_ref, basis_ref, gains_ref, out_state_ref, coef_all_ref, acc, *rest):
        return exchange_kernel(
            last, n_bits, n_ch, part_ref, state_ref, basis_ref, gains_ref, out_state_ref,
            coef_all_ref, acc, rest[:n_bits], *rest[n_bits:]
        )

    dma = pltpu.SemaphoreType.DMA
    vmem = pl.BlockSpec(memory_space=pltpu.VMEM)
    gains, state, coefs = pl.pallas_call(
        body,
        out_shape=(
            jax.ShapeDtypeStruct((2,) + twos + (2 * rows, half), jnp.float32),
            jax.ShapeDtypeStruct(state.shape, jnp.float32),
            jax.ShapeDtypeStruct(coef_shape, jnp.float32),
        ),
        in_specs=[pl.BlockSpec(memory_space=pl.ANY), vmem, vmem],
        out_specs=(vmem, vmem, vmem),
        scratch_shapes=[pltpu.VMEM(partial.shape, jnp.float32)]
        + recv
        + [
            pltpu.VMEM((n_ch, 4, 4 * per, half), jnp.float32),
            dma,
            dma((2, n_bits)),
            dma((2, n_bits)),
            dma((2, n_bits)),
            dma((2, n_bits)),
            dma((n_ch - 1,)),
            dma((n_ch - 1,)),
            dma((2, n_bits)),
            dma((2, n_bits)),
        ],
        compiler_params=pltpu.CompilerParams(
            collective_id=1 if last else 0,
            has_side_effects=True,
            vmem_limit_bytes=40 * 2**20,
        ),
        name="exchange_last" if last else "exchange",
    )(partial, state, basis)
    return gains.reshape((2, n, 2 * rows, half)), state, coefs


def per_device(n, n_ch, vis, model, stations, initial_gains):
    n_dir, n_chan, n_st = initial_gains.shape[1:]
    per = n_dir // n
    half = n_st // 2
    rows = per * n_chan
    chunks = initial_gains.reshape(2, n, rows, 2, half).transpose(3, 1, 0, 2, 4)
    me = lax.axis_index("bl")
    own = lax.dynamic_slice_in_dim(chunks, me, 1, 1).reshape(4, rows, half)
    state = jnp.stack([own, own, jnp.zeros_like(own)])
    gains = chunks.reshape(2, n, 2 * rows, half)
    basis = legendre_basis(SPECTRAL_BINS)
    local = lax.dynamic_slice_in_dim(basis, lax.axis_index("ch") * n_chan, n_chan, 0)
    wide = jnp.broadcast_to(local.T[:, :, None], (4, n_chan, half))
    ids_t = stations.T
    for iteration in range(ITERS):
        partial = local_totals(vis, model, stations, ids_t, gains, n)
        gains, state, coefs = exchange(partial, state, wide, iteration == ITERS - 1, n, n_ch)
    out = gains.reshape(2, n, 2, rows, half).transpose(2, 1, 3, 0, 4)
    out = out.reshape(initial_gains.shape)
    coefs = coefs.reshape(2, n, 4, 2, per, half).transpose(3, 1, 4, 2, 0, 5)
    coefs = coefs.reshape(2, n_dir, 4, 1, n_st)
    consensus = sum(coefs[:, :, k] * local[None, None, :, k, None] for k in range(4))
    return out, consensus


def solution(mesh):
    placed = (
        P(None, "ch", "bl"),
        P(None, None, "ch", "bl"),
        P(None, "bl"),
        P(None, None, "ch", None),
    )
    return jax.shard_map(
        functools.partial(per_device, mesh.shape["bl"], mesh.shape["ch"]),
        mesh=mesh,
        in_specs=placed,
        out_specs=(P(None, None, "ch", None), P(None, None, "ch", None)),
        check_vma=False,
    )
```

```python
import functools

import jax
import jax.numpy as jnp
import numpy as np
from jax import lax
from jax.experimental import pallas as pl
from jax.experimental.pallas import tpu as pltpu
from jax.sharding import PartitionSpec as P

SPECTRAL_BINS = 64
ITERS = 3
penalty = 1.0
MESH = pl.DeviceIdType.MESH
BLOCK = 512


def legendre_basis(channel_count):
    steps = np.arange(channel_count, dtype=np.float32)
    abscissa = np.float32(-1.0) + np.float32(2.0) * steps / np.float32(channel_count - 1)
    columns = []
    for degree in range(4):
        vector = abscissa**degree
        for earlier in columns:
            vector = vector - np.sum(earlier * vector) * earlier
        vector = vector / np.sqrt(np.sum(vector * vector))
        columns.append(vector.astype(np.float32))
    return jnp.asarray(np.stack(columns, axis=1))


def split(value):
    high = value.astype(jnp.bfloat16)
    return high, (value - high.astype(jnp.float32)).astype(jnp.bfloat16)


def totals_kernel(
    n_chunks, n_dir, n_chan, vis_ref, model_ref, row_ref, col_ref, gains_ref, out_ref,
    pieces, gain_l, gain_r, terms, back, accum,
):
    step = pl.program_id(0)
    rows = n_dir * n_chan
    chunk = rows // n_chunks
    block = vis_ref.shape[2]
    n_st = pieces.shape[1]
    half = n_st // 2

    @pl.when(step == 0)
    def _():
        for h in range(2):
            for c in range(n_chunks):
                for part in range(2):
                    high, low = split(gains_ref[h, c, pl.ds(part * chunk, chunk), :])
                    base = part * rows + c * chunk
                    pieces[pl.ds(base, chunk), pl.ds(h * half, half)] = high
                    pieces[pl.ds(2 * rows + base, chunk), pl.ds(h * half, half)] = low

    station = lax.broadcasted_iota(jnp.int32, (n_st, block), 0)
    hot_l = (station == row_ref[0:1, :]).astype(jnp.float32).astype(jnp.bfloat16)
    hot_r = (station == row_ref[1:2, :]).astype(jnp.float32).astype(jnp.bfloat16)
    for side, hot in enumerate((hot_l, hot_r)):
        back[:, pl.ds(pl.multiple_of((step * 2 + side) * block, 128), block)] = hot
    for hot, gain in ((hot_l, gain_l), (hot_r, gain_r)):
        both = jnp.dot(pieces[...], hot, preferred_element_type=jnp.float32)
        gain[...] = both[: 2 * rows] + both[2 * rows :]

    def at(ref, part, d):
        return ref[pl.ds(part * rows + d * n_chan, n_chan), :]

    res_re = vis_ref[0]
    res_im = vis_ref[1]
    for d in range(n_dir):
        m_re, m_im = model_ref[0, d], model_ref[1, d]
        l_re, l_im = at(gain_l, 0, d), at(gain_l, 1, d)
        r_re, r_im = at(gain_r, 0, d), at(gain_r, 1, d)
        a_re = m_re * r_re + m_im * r_im
        a_im = m_im * r_re - m_re * r_im
        res_re = res_re - (l_re * a_re - l_im * a_im)
        res_im = res_im - (l_re * a_im + l_im * a_re)
    for d in range(n_dir):
        m_re, m_im = model_ref[0, d], model_ref[1, d]
        t_re = res_re * m_re + res_im * m_im
        t_im = res_re * m_im - res_im * m_re
        power = m_re * m_re + m_im * m_im
        for side, gain in ((0, gain_r), (1, gain_l)):
            g_re, g_im = at(gain, 0, d), at(gain, 1, d)
            sign = -1.0 if side == 0 else 1.0
            s_im = sign * t_im
            values = (
                t_re * g_re - s_im * g_im,
                t_re * g_im + s_im * g_re,
                power * (g_re * g_re + g_im * g_im),
            )
            for q, value in enumerate(values):
                high, low = split(value)
                base = q * rows + d * n_chan
                terms[pl.ds(base, n_chan), pl.ds(pl.multiple_of((step * 2 + side) * block, 128), block)] = high
                terms[pl.ds(3 * rows + base, n_chan), pl.ds(pl.multiple_of((step * 2 + side) * block, 128), block)] = low

    @pl.when(step == pl.num_programs(0) - 1)
    def _():
        accum[...] = lax.dot_general(
            terms[...], back[...], (((1,), (1,)), ((), ())), preferred_element_type=jnp.float32
        )
        for h in range(2):
            for c in range(n_chunks):
                for q in range(3):
                    base = q * rows + c * chunk
                    out_ref[h, c, pl.ds(q * chunk, chunk), :] = (
                        accum[pl.ds(base, chunk), pl.ds(h * half, half)]
                        + accum[pl.ds(3 * rows + base, chunk), pl.ds(h * half, half)]
                    )


def local_totals(vis, model, ids, ids_t, gains, n_chunks):
    n_dir, n_chan, n_base = model.shape[1:]
    n_st = gains.shape[3] * 2
    rows = n_dir * n_chan
    chunk = rows // n_chunks
    block = min(BLOCK, n_base)
    return pl.pallas_call(
        functools.partial(totals_kernel, n_chunks, n_dir, n_chan),
        grid=(n_base // block,),
        out_shape=jax.ShapeDtypeStruct((2, n_chunks, 3 * chunk, n_st // 2), jnp.float32),
        in_specs=[
            pl.BlockSpec((2, n_chan, block), lambda i: (0, 0, i)),
            pl.BlockSpec((2, n_dir, n_chan, block), lambda i: (0, 0, 0, i)),
            pl.BlockSpec((2, block), lambda i: (0, i)),
            pl.BlockSpec((block, 2), lambda i: (i, 0)),
            pl.BlockSpec(gains.shape, lambda i: (0, 0, 0, 0)),
        ],
        out_specs=pl.BlockSpec((2, n_chunks, 3 * chunk, n_st // 2), lambda i: (0, 0, 0, 0)),
        scratch_shapes=[
            pltpu.VMEM((4 * rows, n_st), jnp.bfloat16),
            pltpu.VMEM((2 * rows, block), jnp.float32),
            pltpu.VMEM((2 * rows, block), jnp.float32),
            pltpu.VMEM((6 * rows, 2 * n_base), jnp.bfloat16),
            pltpu.VMEM((n_st, 2 * n_base), jnp.bfloat16),
            pltpu.VMEM((6 * rows, n_st), jnp.float32),
        ],
        compiler_params=pltpu.CompilerParams(vmem_limit_bytes=56 * 2**20),
        name="station_totals",
    )(vis, model, ids, ids_t, gains)


def orders(n_bits):
    upper = list(range(1, n_bits))
    return ([0] + upper, [0] + upper[::-1])


def exchange_kernel(
    last, n_bits, n_ch, part_ref, state_ref, basis_ref, gains_ref, out_state_ref, coef_all_ref,
    acc, recv, coefs, sem_in, rs_send, rs_recv, ag_send, ag_recv, c_send, c_recv, k_send, k_recv,
):
    n = 2**n_bits
    rows = state_ref.shape[2]
    me = lax.axis_index("bl")
    ch = lax.axis_index("ch")
    bits = [lax.rem(me // (2**k), 2) for k in range(n_bits)]
    partners = [me + (1 - 2 * bits[k]) * (2**k) for k in range(n_bits)]
    load = pltpu.make_async_copy(part_ref, acc, sem_in)
    load.start()

    barrier = pltpu.get_barrier_semaphore()
    for k in range(n_bits):
        pl.semaphore_signal(barrier, inc=1, device_id=(partners[k], ch), device_id_type=MESH)
    for j in range(1, n_ch):
        pl.semaphore_signal(
            barrier, inc=1, device_id=(me, lax.rem(ch + j, n_ch)), device_id_type=MESH
        )
    pl.semaphore_wait(barrier, n_bits + n_ch - 1)
    load.wait()

    order = orders(n_bits)

    def region(stream, stage, flip):
        idx = [slice(None)] * n_bits
        for j in range(stage):
            k = order[stream][j]
            idx[n_bits - 1 - k] = bits[k]
        k = order[stream][stage]
        idx[n_bits - 1 - k] = (1 - bits[k]) if flip else bits[k]
        return (stream,) + tuple(idx)

    def rs_copy(stream, stage):
        k = order[stream][stage]
        slot = recv[stage].at[stream]
        return pltpu.make_async_remote_copy(
            src_ref=acc.at[region(stream, stage, True)],
            dst_ref=slot,
            send_sem=rs_send.at[stream, stage],
            recv_sem=rs_recv.at[stream, stage],
            device_id=(partners[k], ch),
            device_id_type=MESH,
        )

    copies = {}
    for s in range(2):
        copies[s, 0] = rs_copy(s, 0)
        copies[s, 0].start()
    for stage in range(n_bits):
        for s in range(2):
            copies[s, stage].wait_recv()
            where = region(s, stage, False)
            acc[where] = acc[where] + recv[stage][s]
            if stage + 1 < n_bits:
                copies[s, stage + 1] = rs_copy(s, stage + 1)
                copies[s, stage + 1].start()

    mine = tuple(bits[n_bits - 1 - i] for i in range(n_bits))

    def gather_copy(buf, sends, recvs, stream, stage):
        k = order[stream][stage]
        idx = [slice(None)] * n_bits
        for j in range(stage + 1):
            kk = order[stream][j]
            idx[n_bits - 1 - kk] = bits[kk]
        where = (stream,) + tuple(idx)
        return pltpu.make_async_remote_copy(
            src_ref=buf.at[where],
            dst_ref=buf.at[where],
            send_sem=sends.at[stream, stage],
            recv_sem=recvs.at[stream, stage],
            device_id=(partners[k], ch),
            device_id_type=MESH,
        )

    gathers = {}
    shifted = []
    for s in range(2):
        totals = acc[(s,) + mine]
        weight = totals[2 * rows :]
        factor = 1.0 / (weight + penalty)
        for part in range(2):
            gain = state_ref[0, s * 2 + part]
            cons = state_ref[1, s * 2 + part]
            dual = state_ref[2, s * 2 + part]
            numerator = totals[part * rows : (part + 1) * rows] + gain * weight
            new = (numerator + penalty * (cons - dual)) * factor
            gains_ref[(s,) + mine + (pl.ds(part * rows, rows),)] = new
            out_state_ref[0, s * 2 + part] = new
            shifted.append(new + dual)
        gathers[s, n_bits - 1] = gather_copy(gains_ref, ag_send, ag_recv, s, n_bits - 1)
        gathers[s, n_bits - 1].start()

    n_chan = basis_ref.shape[1]
    per = rows // n_chan
    for k in range(4):
        pieces = []
        for value in shifted:
            for i in range(per):
                pieces.append(
                    jnp.sum(
                        value[i * n_chan : (i + 1) * n_chan] * basis_ref[k], axis=0, keepdims=True
                    )
                )
        for r, piece in enumerate(pieces):
            coefs[0, k, pl.ds(r, 1), :] = piece
    sends = []
    for j in range(1, n_ch):
        copy = pltpu.make_async_remote_copy(
            src_ref=coefs.at[0],
            dst_ref=coefs.at[j],
            send_sem=c_send.at[j - 1],
            recv_sem=c_recv.at[j - 1],
            device_id=(me, lax.rem(ch + j, n_ch)),
            device_id_type=MESH,
        )
        copy.start()
        sends.append(copy)

    def advance(buf, sends, recvs, table, stage):
        for s in range(2):
            table[s, stage].wait_recv()
            if stage > 0:
                table[s, stage - 1] = gather_copy(buf, sends, recvs, s, stage - 1)
                table[s, stage - 1].start()

    advance(gains_ref, ag_send, ag_recv, gathers, n_bits - 1)
    for copy in sends:
        copy.wait_recv()
    total = [None] * 4
    for k in range(4):
        value = coefs[0, k]
        for j in range(1, n_ch):
            value = value + coefs[j, k]
        total[k] = value
    k_gathers = {}
    if last:
        for s in range(2):
            for k in range(4):
                coef_all_ref[(s,) + mine + (k,)] = total[k][s * 2 * per : (s + 1) * 2 * per]
            k_gathers[s, n_bits - 1] = gather_copy(coef_all_ref, k_send, k_recv, s, n_bits - 1)
            k_gathers[s, n_bits - 1].start()
        out_state_ref[1] = out_state_ref[0]
        out_state_ref[2] = out_state_ref[0]
    else:
        coef_all_ref[...] = jnp.zeros_like(coef_all_ref)
        for index, value in enumerate(shifted):
            for i in range(per):
                fit = total[0][index * per + i : index * per + i + 1] * basis_ref[0]
                for k in range(1, 4):
                    fit = fit + total[k][index * per + i : index * per + i + 1] * basis_ref[k]
                where = pl.ds(i * n_chan, n_chan)
                out_state_ref[1, index, where, :] = fit
                out_state_ref[2, index, where, :] = value[i * n_chan : (i + 1) * n_chan] - fit
    for stage in range(n_bits - 2, -1, -1):
        advance(gains_ref, ag_send, ag_recv, gathers, stage)
        if last:
            advance(coef_all_ref, k_send, k_recv, k_gathers, stage + 1)
    if last:
        advance(coef_all_ref, k_send, k_recv, k_gathers, 0)

    for table in (copies, gathers, k_gathers):
        for copy in table.values():
            copy.wait_send()
    for copy in sends:
        copy.wait_send()


def exchange(partial, state, basis, last, n, n_ch):
    n_bits = n.bit_length() - 1
    rows, half = state.shape[2:]
    n_chan = basis.shape[1]
    per = rows // n_chan
    twos = (2,) * n_bits
    partial = partial.reshape((2,) + twos + partial.shape[2:])
    coef_shape = (2,) + ((twos) if last else (1,) * n_bits) + (4, 2 * per, half)
    recv = [
        pltpu.VMEM((2,) + (2,) * (n_bits - 1 - stage) + (3 * rows, half), jnp.float32)
        for stage in range(n_bits)
    ]

    def body(part_ref, state_ref, basis_ref, gains_ref, out_state_ref, coef_all_ref, acc, *rest):
        return exchange_kernel(
            last, n_bits, n_ch, part_ref, state_ref, basis_ref, gains_ref, out_state_ref,
            coef_all_ref, acc, rest[:n_bits], *rest[n_bits:]
        )

    dma = pltpu.SemaphoreType.DMA
    vmem = pl.BlockSpec(memory_space=pltpu.VMEM)
    gains, state, coefs = pl.pallas_call(
        body,
        out_shape=(
            jax.ShapeDtypeStruct((2,) + twos + (2 * rows, half), jnp.float32),
            jax.ShapeDtypeStruct(state.shape, jnp.float32),
            jax.ShapeDtypeStruct(coef_shape, jnp.float32),
        ),
        in_specs=[pl.BlockSpec(memory_space=pl.ANY), vmem, vmem],
        out_specs=(vmem, vmem, vmem),
        scratch_shapes=[pltpu.VMEM(partial.shape, jnp.float32)]
        + recv
        + [
            pltpu.VMEM((n_ch, 4, 4 * per, half), jnp.float32),
            dma,
            dma((2, n_bits)),
            dma((2, n_bits)),
            dma((2, n_bits)),
            dma((2, n_bits)),
            dma((n_ch - 1,)),
            dma((n_ch - 1,)),
            dma((2, n_bits)),
            dma((2, n_bits)),
        ],
        compiler_params=pltpu.CompilerParams(
            collective_id=1 if last else 0,
            has_side_effects=True,
            vmem_limit_bytes=40 * 2**20,
        ),
        name="exchange_last" if last else "exchange",
    )(partial, state, basis)
    return gains.reshape((2, n, 2 * rows, half)), state, coefs


def per_device(n, n_ch, vis, model, stations, initial_gains):
    n_dir, n_chan, n_st = initial_gains.shape[1:]
    per = n_dir // n
    half = n_st // 2
    rows = per * n_chan
    chunks = initial_gains.reshape(2, n, rows, 2, half).transpose(3, 1, 0, 2, 4)
    me = lax.axis_index("bl")
    own = lax.dynamic_slice_in_dim(chunks, me, 1, 1).reshape(4, rows, half)
    state = jnp.stack([own, own, jnp.zeros_like(own)])
    gains = chunks.reshape(2, n, 2 * rows, half)
    basis = legendre_basis(SPECTRAL_BINS)
    local = lax.dynamic_slice_in_dim(basis, lax.axis_index("ch") * n_chan, n_chan, 0)
    wide = jnp.broadcast_to(local.T[:, :, None], (4, n_chan, half))
    ids_t = stations.T
    for iteration in range(ITERS):
        partial = local_totals(vis, model, stations, ids_t, gains, n)
        gains, state, coefs = exchange(partial, state, wide, iteration == ITERS - 1, n, n_ch)
    out = gains.reshape(2, n, 2, rows, half).transpose(2, 1, 3, 0, 4)
    out = out.reshape(initial_gains.shape)
    coefs = coefs.reshape(2, n, 4, 2, per, half).transpose(3, 1, 4, 2, 0, 5)
    coefs = coefs.reshape(2, n_dir, 4, 1, n_st)
    consensus = sum(coefs[:, :, k] * local[None, None, :, k, None] for k in range(4))
    return out, consensus


def solution(mesh):
    placed = (
        P(None, "ch", "bl"),
        P(None, None, "ch", "bl"),
        P(None, "bl"),
        P(None, None, "ch", None),
    )
    return jax.shard_map(
        functools.partial(per_device, mesh.shape["bl"], mesh.shape["ch"]),
        mesh=mesh,
        in_specs=placed,
        out_specs=(P(None, None, "ch", None), P(None, None, "ch", None)),
        check_vma=False,
    )
```
